32 devices in a mesh: st: 8 (over z, y), ob: 4 (over x, core).
Axes of the slice: x: 2, y: 2, z: 4, core: 2. Of those that a mesh axis runs over, the one named last changes fastest.
Arguments:
- ensemble: bfloat16 [18432, 64], P('st'), may hold values from -3 to 3
- weights: bfloat16 [4096, 64], P('ob'), may hold values from -6 to 6
- obs_column: int32 [4096], P('ob'), may hold values from 0 to 18431
Outputs:
- forecast: float32 [64, 3, 48, 128], P('ob', None, 'st')
The draws below stay inside these ranges and needn't reach their ends.
All inputs are finite; a program needn't handle non-finite values.
Results may differ from the reference program's by a relative error of at most 0.0061.
Values may be sent and summed in bfloat16 or wider, within the bound.
A program may use at most 128 MiB of HBM per device.

```python
import jax
import jax.numpy as jnp
from jax import lax

NLON = 128
STEPS = 3
OBS_DEV = 1024
NLAT = 48
STATE = 18432
OBS = 4096
MEMBERS = 64
RADIUS = 48
N_OB = 4


def with_ends(entries, own_key, smallest, largest):
    longest = entries.shape.index(max(entries.shape))
    spots = []
    for shift in (0, 1):
        where = [jax.random.randint(jax.random.fold_in(own_key, axis), (), 0, length) for axis, length in enumerate(entries.shape)]
        where[longest] = (where[longest] + shift) % entries.shape[longest]
        spots.append(tuple(where))
    return entries.at[spots[0]].set(smallest).at[spots[1]].set(largest)


def block_levels(own_key, shape, shards, least, top_value):
    loudness = 1.0
    for position, shards_of in shards:
        steps = jax.random.uniform(jax.random.fold_in(jax.random.fold_in(own_key, 6), position), (shards_of,), jnp.float32, least / len(shards), top_value / len(shards))
        loudness = loudness * jnp.repeat(jnp.exp(steps), shape[position] // shards_of).reshape((-1,) + (1,) * (len(shape) - 1 - position))
    return loudness


def gaussian(stream_key, shape, deviation, most, split=(), held_as=jnp.bfloat16):
    values = deviation * jax.random.normal(stream_key, shape, jnp.float32)
    if split:
        values = values * block_levels(stream_key, shape, split, -0.22, 0.18)
    return jnp.clip(values, -most, most).astype(held_as)


def setup_inputs(seed: int = 0) -> dict:
    key_list = jax.random.split(jax.random.key(seed), 4)
    return {
        "ensemble": gaussian(key_list[0], (STATE, MEMBERS), 0.5, 3.0, ((0, 8),)),
        "weights": gaussian(key_list[1], (OBS, MEMBERS), 1.0, 6.0, ((0, 4),)),
        "obs_column": with_ends(jax.random.randint(key_list[2], (OBS,), 0, STATE), jax.random.fold_in(key_list[2], 1), 0, STATE - 1).astype(jnp.int32),
    }


time_step = 0.3


def tapering(state_rows, columns):
    state_lat = state_rows // (3 * NLON)
    state_lon = state_rows % NLON
    obs_lat = columns // (3 * NLON)
    obs_lon = columns % NLON
    lat_gap = state_lat[:, None] - obs_lat[None, :]
    lon_gap = jnp.abs(state_lon[:, None] - obs_lon[None, :])
    lon_gap = jnp.minimum(lon_gap, NLON - lon_gap)
    squared = (lat_gap * lat_gap + lon_gap * lon_gap).astype(jnp.float32)
    falloff = jnp.maximum(jnp.float32(0.0), 1.0 - squared / jnp.float32(RADIUS * RADIUS))
    return falloff * falloff


def advance(padded, latitude, lat_count):
    centre = padded[:, :, 1:-1]
    northern = padded[:, :, 2:]
    southern = padded[:, :, :-2]
    eastern = jnp.roll(centre, -1, axis=3)
    western = jnp.roll(centre, 1, axis=3)
    flux_east = (1.0 + padded[:, 0]) * padded[:, 1]
    flux_north = (1.0 + padded[:, 0]) * padded[:, 2]
    mid_east = flux_east[:, 1:-1]
    divergence = (jnp.roll(mid_east, -1, axis=2) - jnp.roll(mid_east, 1, axis=2)) / 2.0
    divergence = divergence + (flux_north[:, 2:] - flux_north[:, :-2]) / 2.0
    along_lon = (eastern - western) / 2.0
    along_lat = (northern - southern) / 2.0
    eastward = centre[:, 1]
    northward = centre[:, 2]
    coriolis = 0.8 * jnp.sin(jnp.pi * ((latitude.astype(jnp.float32) + 0.5) / lat_count - 0.5))
    coriolis = coriolis[None, :, None]
    tend_east = eastward * along_lon[:, 1] + northward * along_lat[:, 1] + along_lon[:, 0] - coriolis * northward
    tend_north = eastward * along_lon[:, 2] + northward * along_lat[:, 2] + along_lat[:, 0] + coriolis * eastward
    tendency = jnp.stack([divergence, tend_east, tend_north], axis=1)
    return 0.25 * (northern + southern + eastern + western) - time_step * tendency


def reference(ensemble, weights, obs_column):
    members = ensemble.shape[1]
    predicted_rows = ensemble.astype(jnp.float32)
    ensemble_mean = jnp.mean(predicted_rows, axis=1, keepdims=True)
    member_anomalies = (predicted_rows - ensemble_mean).astype(jnp.bfloat16)
    obs_anom = member_anomalies[obs_column]
    state_rows = jnp.arange(STATE, dtype=jnp.int32)
    column_blocks = obs_column.reshape(N_OB, OBS_DEV)
    anom_blocks = obs_anom.reshape(N_OB, OBS_DEV, members)
    weight_blocks = weights.reshape(N_OB, OBS_DEV, members)

    def obs_block(running, pieces):
        columns, block_anom, block_weights = pieces
        covariance = jnp.dot(member_anomalies, block_anom.T, preferred_element_type=jnp.float32)
        kalman_gain = (covariance * tapering(state_rows, columns) / jnp.float32(members - 1)).astype(jnp.bfloat16)
        return running + jnp.dot(kalman_gain, block_weights, preferred_element_type=jnp.float32), None

    state_update, _ = lax.scan(obs_block, jnp.zeros((STATE, members), jnp.float32), (column_blocks, anom_blocks, weight_blocks))
    updated_members = predicted_rows + state_update
    fields = updated_members.reshape(NLAT, 3, NLON, members).transpose(3, 1, 0, 2)
    latitude = jnp.arange(NLAT, dtype=jnp.int32)
    for section in range(STEPS):
        padded = jnp.pad(fields, ((0, 0), (0, 0), (1, 1), (0, 0)))
        fields = advance(padded, latitude, NLAT)
    return fields
```

```python
import functools

import jax
import jax.numpy as jnp
import numpy as np
from jax import lax
from jax.experimental import pallas as pl
from jax.experimental.pallas import tpu as pltpu
from jax.sharding import PartitionSpec as P

NLON = 128
FIELDS = 3
STEPS = 3
MESH = pl.DeviceIdType.MESH
time_step = 0.3
F32 = jnp.float32
BF16 = jnp.bfloat16


def remote(src, dst, send, recv, device):
    return pltpu.make_async_remote_copy(
        src_ref=src, dst_ref=dst, send_sem=send, recv_sem=recv, device_id=device, device_id_type=MESH
    )


def analysis_kernel(
    n_st, n_ob, ens_ref, w_ref, col_ref, out_ref,
    anom_t, anom, own, picked, part, gathered, obs_t, taper, inc, inc_send, inc_recv,
    p_send, p_recv, g_send, g_recv, i_send, i_recv, h_send, h_recv,
):
    st, ob = lax.axis_index("st"), lax.axis_index("ob")
    rows, members = ens_ref.shape
    obs = w_ref.shape[0]
    per = members // n_ob
    lats = rows // (FIELDS * NLON)
    blocks = rows // NLON
    chunk = obs // n_st
    radius2 = float((lats * n_st) ** 2)

    barrier = pltpu.get_barrier_semaphore()
    for d in range(1, n_st):
        pl.semaphore_signal(barrier, inc=1, device_id={"st": lax.rem(st + d, n_st)}, device_id_type=MESH)
    for d in range(1, n_ob):
        pl.semaphore_signal(barrier, inc=1, device_id={"ob": lax.rem(ob + d, n_ob)}, device_id_type=MESH)

    for b in range(blocks):
        e_t = ens_ref[b * NLON:(b + 1) * NLON, :].astype(F32).T
        mean = jnp.sum(e_t, axis=0, keepdims=True) / members
        anom_t[:, b * NLON:(b + 1) * NLON] = (e_t - mean).astype(BF16)
        own[:, b] = e_t.reshape(n_ob, per, NLON)

    column = col_ref[...]
    depth = 2 * FIELDS * NLON if lats % 2 == 0 else FIELDS * NLON
    relative = column - st * rows
    spot = lax.broadcasted_iota(jnp.int32, (depth, obs), 0)
    total = jnp.zeros((members, obs), F32)
    for k in range(rows // depth):
        hot = jnp.where(spot == relative - k * depth, F32(1.0), F32(0.0)).astype(BF16)
        total = total + jnp.dot(anom_t[:, k * depth:(k + 1) * depth], hot, preferred_element_type=F32)
    total = total.astype(BF16)
    for c in range(n_st):
        picked[c] = total[:, c * chunk:(c + 1) * chunk]

    pl.semaphore_wait(barrier, n_st - 1 + n_ob - 1)

    first = []
    for d in range(1, n_st):
        peer = lax.rem(st + d, n_st)
        first.append(remote(picked.at[peer], part.at[d], p_send.at[d], p_recv.at[d], {"st": peer}))
    for copy in first:
        copy.start()

    ones = jnp.ones((members, members), BF16)
    for l in range(lats):
        band = slice(l * FIELDS * NLON, (l + 1) * FIELDS * NLON)
        e = ens_ref[band, :]
        mean = jnp.dot(e, ones, preferred_element_type=F32) / members
        anom[l] = (e.astype(F32) - mean).astype(BF16)
    obs_lat = jnp.floor((column.astype(F32) + 0.5) * (1.0 / (FIELDS * NLON)))
    obs_lon = (column & (NLON - 1)).astype(F32)
    lon = lax.broadcasted_iota(jnp.int32, (NLON, obs), 0).astype(F32)
    lon_gap = jnp.abs(lon - obs_lon)
    lon_gap = jnp.minimum(lon_gap, NLON - lon_gap)
    lon_left = radius2 - lon_gap * lon_gap
    scale = 1.0 / (radius2 * radius2 * (members - 1))
    for l in range(lats):
        lat_gap = obs_lat - (st * lats + l).astype(F32)
        fall = jnp.maximum(lon_left - lat_gap * lat_gap, 0.0)
        taper[l] = fall * (fall * scale)

    for copy in first:
        copy.wait_recv()
    mine = picked[st].astype(F32)
    for d in range(1, n_st):
        mine = mine + part[d].astype(F32)
    gathered[st] = mine.astype(BF16)

    second = []
    for d in range(1, n_st):
        peer = lax.rem(st + d, n_st)
        second.append(remote(gathered.at[st], gathered.at[st], g_send.at[d], g_recv.at[d], {"st": peer}))
    for copy in second:
        copy.start()
    for copy in second:
        copy.wait_recv()
    for c in range(n_st):
        obs_t[:, c * chunk:(c + 1) * chunk] = gathered[c]

    width = min(256, obs)

    def sends(l):
        return [
            remote(
                inc_send.at[lax.rem(ob + d, n_ob), l], inc_recv.at[d, l],
                i_send.at[d, l], i_recv.at[d, l], {"ob": lax.rem(ob + d, n_ob)},
            )
            for d in range(1, n_ob)
        ]

    def latitude(l, carry):
        total = jnp.zeros((FIELDS * NLON, members), F32)
        a = anom[l]
        for k in range(obs // width):
            at = slice(k * width, (k + 1) * width)
            cov = jnp.dot(a, obs_t[:, at], preferred_element_type=F32)
            gain = cov.reshape(FIELDS, NLON, width) * taper[l, :, at][None]
            gain = gain.astype(BF16).reshape(FIELDS * NLON, width)
            total = total + jnp.dot(gain, w_ref[at, :], preferred_element_type=F32)
        for f in range(FIELDS):
            turned = total[f * NLON:(f + 1) * NLON, :].T.reshape(n_ob, per, NLON)
            inc[:, l, f] = turned
            inc_send[:, l, f] = turned.astype(BF16)
        for copy in sends(l):
            copy.start()
        return carry

    lax.fori_loop(0, lats, latitude, 0)

    for l in range(lats):
        for copy in sends(l):
            copy.wait_recv()
        for f in range(FIELDS):
            value = own[ob, l * FIELDS + f] + inc[ob, l, f]
            for d in range(1, n_ob):
                value = value + inc_recv[d, l, f].astype(F32)
            out_ref[STEPS + l, f] = value

    up = remote(
        out_ref.at[pl.ds(lats, STEPS)], out_ref.at[pl.ds(0, STEPS)],
        h_send.at[0], h_recv.at[0], {"st": lax.rem(st + 1, n_st)},
    )
    down = remote(
        out_ref.at[pl.ds(STEPS, STEPS)], out_ref.at[pl.ds(STEPS + lats, STEPS)],
        h_send.at[1], h_recv.at[1], {"st": lax.rem(st + n_st - 1, n_st)},
    )

    @pl.when(st < n_st - 1)
    def _():
        up.start()

    @pl.when(st > 0)
    def _():
        down.start()

    @pl.when(st == 0)
    def _():
        out_ref[0:STEPS] = jnp.zeros((STEPS,) + out_ref.shape[1:], F32)

    @pl.when(st == n_st - 1)
    def _():
        out_ref[STEPS + lats:] = jnp.zeros((STEPS,) + out_ref.shape[1:], F32)

    for copy in first + second:
        copy.wait_send()
    for l in range(lats):
        for copy in sends(l):
            copy.wait_send()

    @pl.when(st < n_st - 1)
    def _():
        up.wait_send()
        down.wait_recv()

    @pl.when(st > 0)
    def _():
        down.wait_send()
        up.wait_recv()


def forecast_kernel(n_st, coriolis_ref, ext_ref, out_ref):
    st = lax.axis_index("st")
    lats = ext_ref.shape[0] - 2 * STEPS
    lat_count = lats * n_st

    def east(q):
        return pltpu.roll(q, NLON - 1, 2)

    def west(q):
        return pltpu.roll(q, 1, 2)

    h, u, v = (ext_ref[:, f] for f in range(FIELDS))
    for step in range(STEPS):
        flux_east = (1.0 + h[1:-1]) * u[1:-1]
        flux_north = (1.0 + h) * v
        around, dlon, dlat = [], [], []
        for q in (h, u, v):
            c = q[1:-1]
            e, w, n, s = east(c), west(c), q[2:], q[:-2]
            around.append(0.25 * (n + s + e + w))
            dlon.append((e - w) * 0.5)
            dlat.append((n - s) * 0.5)
        divergence = (east(flux_east) - west(flux_east)) * 0.5 + (flux_north[2:] - flux_north[:-2]) * 0.5
        cu, cv = u[1:-1], v[1:-1]
        count = cu.shape[0]
        base = st * lats - STEPS + step + 1
        new = [[], [], []]
        for i in range(count):
            latitude = base + i
            inside = (latitude >= 0) & (latitude < lat_count)
            keep = jnp.where(inside, F32(1.0), F32(0.0))
            turn = coriolis_ref[0, jnp.clip(latitude, 0, lat_count - 1)]
            tend_u = cu[i] * dlon[1][i] + cv[i] * dlat[1][i] + dlon[0][i] - turn * cv[i]
            tend_v = cu[i] * dlon[2][i] + cv[i] * dlat[2][i] + dlat[0][i] + turn * cu[i]
            for f, tend in enumerate((divergence[i], tend_u, tend_v)):
                value = around[f][i] - time_step * tend
                if step < STEPS - 1:
                    new[f].append(jnp.where(keep > 0.5, value, 0.0))
                else:
                    out_ref[:, f, i, :] = value
        if step < STEPS - 1:
            h, u, v = (jnp.stack(q) for q in new)


def local(n_st, n_ob, ensemble, weights, obs_column):
    rows, members = ensemble.shape
    obs = weights.shape[0]
    per = members // n_ob
    lats = rows // (FIELDS * NLON)
    blocks = rows // NLON
    chunk = obs // n_st
    vmem = pl.BlockSpec(memory_space=pltpu.VMEM)
    dma = pltpu.SemaphoreType.DMA
    ext = pl.pallas_call(
        functools.partial(analysis_kernel, n_st, n_ob),
        out_shape=jax.ShapeDtypeStruct((lats + 2 * STEPS, FIELDS, per, NLON), F32),
        in_specs=[vmem] * 3,
        out_specs=vmem,
        scratch_shapes=[
            pltpu.VMEM((members, rows), BF16),
            pltpu.VMEM((lats, FIELDS * NLON, members), BF16),
            pltpu.VMEM((n_ob, blocks, per, NLON), F32),
            pltpu.VMEM((n_st, members, chunk), BF16),
            pltpu.VMEM((n_st, members, chunk), BF16),
            pltpu.VMEM((n_st, members, chunk), BF16),
            pltpu.VMEM((members, obs), BF16),
            pltpu.VMEM((lats, NLON, obs), F32),
            pltpu.VMEM((n_ob, lats, FIELDS, per, NLON), F32),
            pltpu.VMEM((n_ob, lats, FIELDS, per, NLON), BF16),
            pltpu.VMEM((n_ob, lats, FIELDS, per, NLON), BF16),
            dma((n_st,)), dma((n_st,)), dma((n_st,)), dma((n_st,)),
            dma((n_ob, lats)), dma((n_ob, lats)), dma((2,)), dma((2,)),
        ],
        compiler_params=pltpu.CompilerParams(
            collective_id=0, has_side_effects=True, vmem_limit_bytes=48 * 1024 * 1024
        ),
        name="analysis",
    )(ensemble, weights, obs_column.reshape(1, obs))
    lat_count = lats * n_st
    degrees = (np.arange(lat_count, dtype=np.float32) + 0.5) / lat_count - 0.5
    coriolis = (0.8 * np.sin(np.pi * degrees)).astype(np.float32).reshape(1, lat_count)
    return pl.pallas_call(
        functools.partial(forecast_kernel, n_st),
        out_shape=jax.ShapeDtypeStruct((per, FIELDS, lats, NLON), F32),
        in_specs=[pl.BlockSpec(memory_space=pltpu.SMEM), vmem],
        out_specs=vmem,
        name="forecast",
    )(jnp.asarray(coriolis), ext)


def solution(mesh):
    return jax.shard_map(
        functools.partial(local, mesh.shape["st"], mesh.shape["ob"]),
        mesh=mesh,
        in_specs=(P("st", None), P("ob", None), P("ob")),
        out_specs=P("ob", None, "st", None),
        check_vma=False,
    )
```

```python
import functools

import jax
import jax.numpy as jnp
import numpy as np
from jax import lax
from jax.experimental import pallas as pl
from jax.experimental.pallas import tpu as pltpu
from jax.sharding import PartitionSpec as P

NLON = 128
FIELDS = 3
STEPS = 3
MESH = pl.DeviceIdType.MESH
time_step = 0.3
F32 = jnp.float32
BF16 = jnp.bfloat16


def remote(src, dst, send, recv, device):
    return pltpu.make_async_remote_copy(
        src_ref=src, dst_ref=dst, send_sem=send, recv_sem=recv, device_id=device, device_id_type=MESH
    )


def analysis_kernel(
    n_st, n_ob, ens_hbm, w_hbm, col_hbm, out_ref, ens_ref, w_ref, col_ref, loaded,
    anom_t, anom, w, picked, part, gathered, obs_t, taper, inc, inc_send, inc_recv,
    p_send, p_recv, g_send, g_recv, i_send, i_recv, h_send, h_recv,
):
    st, ob = lax.axis_index("st"), lax.axis_index("ob")
    members, rows = ens_ref.shape
    obs = w_ref.shape[1]
    per = members // n_ob
    lats = rows // (FIELDS * NLON)
    blocks = rows // NLON
    chunk = obs // n_st
    radius2 = float((lats * n_st) ** 2)

    loads = [
        pltpu.make_async_copy(src, dst, loaded.at[i])
        for i, (src, dst) in enumerate(((ens_hbm, ens_ref), (col_hbm, col_ref), (w_hbm, w_ref)))
    ]
    for load in loads:
        load.start()
    barrier = pltpu.get_barrier_semaphore()
    for d in range(1, n_st):
        pl.semaphore_signal(barrier, inc=1, device_id={"st": lax.rem(st + d, n_st)}, device_id_type=MESH)
    for d in range(1, n_ob):
        pl.semaphore_signal(barrier, inc=1, device_id={"ob": lax.rem(ob + d, n_ob)}, device_id_type=MESH)

    loads[0].wait()
    for b in range(blocks):
        e_t = ens_ref[:, b * NLON:(b + 1) * NLON].astype(F32)
        mean = jnp.sum(e_t, axis=0, keepdims=True) / members
        anom_t[:, b * NLON:(b + 1) * NLON] = (e_t - mean).astype(BF16)

    loads[1].wait()
    column = col_ref[...]
    depth = 2 * FIELDS * NLON if lats % 2 == 0 else FIELDS * NLON
    relative = column - st * rows
    spot = lax.broadcasted_iota(jnp.int32, (depth, obs), 0)
    total = jnp.zeros((members, obs), F32)
    for k in range(rows // depth):
        hot = jnp.where(spot == relative - k * depth, F32(1.0), F32(0.0)).astype(BF16)
        total = total + jnp.dot(anom_t[:, k * depth:(k + 1) * depth], hot, preferred_element_type=F32)
    total = total.astype(BF16)
    for c in range(n_st):
        picked[c] = total[:, c * chunk:(c + 1) * chunk]

    pl.semaphore_wait(barrier, n_st - 1 + n_ob - 1)

    first = []
    for d in range(1, n_st):
        peer = lax.rem(st + d, n_st)
        first.append(remote(picked.at[peer], part.at[d], p_send.at[d], p_recv.at[d], {"st": peer}))
    for copy in first:
        copy.start()

    for b in range(blocks):
        l, f = divmod(b, FIELDS)
        block = anom_t[:, b * NLON:(b + 1) * NLON].astype(F32)
        anom[l, f * NLON:(f + 1) * NLON, :] = block.T.astype(BF16)
    loads[2].wait()
    for b in range(obs // NLON):
        at = slice(b * NLON, (b + 1) * NLON)
        w[at, :] = w_ref[:, at].astype(F32).T.astype(BF16)
    obs_lat = jnp.floor((column.astype(F32) + 0.5) * (1.0 / (FIELDS * NLON)))
    obs_lon = (column & (NLON - 1)).astype(F32)
    lon = lax.broadcasted_iota(jnp.int32, (NLON, obs), 0).astype(F32)
    lon_gap = jnp.abs(lon - obs_lon)
    lon_gap = jnp.minimum(lon_gap, NLON - lon_gap)
    lon_left = radius2 - lon_gap * lon_gap
    scale = 1.0 / (radius2 * radius2 * (members - 1))
    for l in range(lats):
        lat_gap = obs_lat - (st * lats + l).astype(F32)
        fall = jnp.maximum(lon_left - lat_gap * lat_gap, 0.0)
        taper[l] = fall * (fall * scale)

    for copy in first:
        copy.wait_recv()
    mine = picked[st].astype(F32)
    for d in range(1, n_st):
        mine = mine + part[d].astype(F32)
    gathered[st] = mine.astype(BF16)

    second = []
    for d in range(1, n_st):
        peer = lax.rem(st + d, n_st)
        second.append(remote(gathered.at[st], gathered.at[st], g_send.at[d], g_recv.at[d], {"st": peer}))
    for copy in second:
        copy.start()
    for copy in second:
        copy.wait_recv()
    for c in range(n_st):
        obs_t[:, c * chunk:(c + 1) * chunk] = gathered[c]

    width = min(256, obs)

    def sends(l):
        return [
            remote(
                inc_send.at[lax.rem(ob + d, n_ob), l], inc_recv.at[d, l],
                i_send.at[d, l], i_recv.at[d, l], {"ob": lax.rem(ob + d, n_ob)},
            )
            for d in range(1, n_ob)
        ]

    def latitude(l, carry):
        total = jnp.zeros((FIELDS * NLON, members), F32)
        a = anom[l]
        for k in range(obs // width):
            at = slice(k * width, (k + 1) * width)
            cov = jnp.dot(a, obs_t[:, at], preferred_element_type=F32)
            gain = cov.reshape(FIELDS, NLON, width) * taper[l, :, at][None]
            gain = gain.astype(BF16).reshape(FIELDS * NLON, width)
            total = total + jnp.dot(gain, w[at, :], preferred_element_type=F32)
        for f in range(FIELDS):
            turned = total[f * NLON:(f + 1) * NLON, :].T.reshape(n_ob, per, NLON)
            inc[:, l, f] = turned
            inc_send[:, l, f] = turned.astype(BF16)
        for copy in sends(l):
            copy.start()
        return carry

    lax.fori_loop(0, lats, latitude, 0)

    own = ens_ref[pl.ds(pl.multiple_of(ob * per, per), per), :].astype(F32)
    for l in range(lats):
        for copy in sends(l):
            copy.wait_recv()
        for f in range(FIELDS):
            value = own[:, (l * FIELDS + f) * NLON:(l * FIELDS + f + 1) * NLON] + inc[ob, l, f]
            for d in range(1, n_ob):
                value = value + inc_recv[d, l, f].astype(F32)
            out_ref[STEPS + l, f] = value

    up = remote(
        out_ref.at[pl.ds(lats, STEPS)], out_ref.at[pl.ds(0, STEPS)],
        h_send.at[0], h_recv.at[0], {"st": lax.rem(st + 1, n_st)},
    )
    down = remote(
        out_ref.at[pl.ds(STEPS, STEPS)], out_ref.at[pl.ds(STEPS + lats, STEPS)],
        h_send.at[1], h_recv.at[1], {"st": lax.rem(st + n_st - 1, n_st)},
    )

    @pl.when(st < n_st - 1)
    def _():
        up.start()

    @pl.when(st > 0)
    def _():
        down.start()

    @pl.when(st == 0)
    def _():
        out_ref[0:STEPS] = jnp.zeros((STEPS,) + out_ref.shape[1:], F32)

    @pl.when(st == n_st - 1)
    def _():
        out_ref[STEPS + lats:] = jnp.zeros((STEPS,) + out_ref.shape[1:], F32)

    for copy in first + second:
        copy.wait_send()
    for l in range(lats):
        for copy in sends(l):
            copy.wait_send()

    @pl.when(st < n_st - 1)
    def _():
        up.wait_send()
        down.wait_recv()

    @pl.when(st > 0)
    def _():
        down.wait_send()
        up.wait_recv()


def forecast_kernel(n_st, coriolis_ref, ext_ref, out_ref):
    st = lax.axis_index("st")
    lats = ext_ref.shape[0] - 2 * STEPS
    lat_count = lats * n_st

    def east(q):
        return pltpu.roll(q, NLON - 1, 2)

    def west(q):
        return pltpu.roll(q, 1, 2)

    h, u, v = (ext_ref[:, f] for f in range(FIELDS))
    for step in range(STEPS):
        flux_east = (1.0 + h[1:-1]) * u[1:-1]
        flux_north = (1.0 + h) * v
        around, dlon, dlat = [], [], []
        for q in (h, u, v):
            c = q[1:-1]
            e, w, n, s = east(c), west(c), q[2:], q[:-2]
            around.append(0.25 * (n + s + e + w))
            dlon.append((e - w) * 0.5)
            dlat.append((n - s) * 0.5)
        divergence = (east(flux_east) - west(flux_east)) * 0.5 + (flux_north[2:] - flux_north[:-2]) * 0.5
        cu, cv = u[1:-1], v[1:-1]
        count = cu.shape[0]
        base = st * lats - STEPS + step + 1
        new = [[], [], []]
        for i in range(count):
            latitude = base + i
            inside = (latitude >= 0) & (latitude < lat_count)
            keep = jnp.where(inside, F32(1.0), F32(0.0))
            turn = coriolis_ref[0, jnp.clip(latitude, 0, lat_count - 1)]
            tend_u = cu[i] * dlon[1][i] + cv[i] * dlat[1][i] + dlon[0][i] - turn * cv[i]
            tend_v = cu[i] * dlon[2][i] + cv[i] * dlat[2][i] + dlat[0][i] + turn * cu[i]
            for f, tend in enumerate((divergence[i], tend_u, tend_v)):
                value = around[f][i] - time_step * tend
                if step < STEPS - 1:
                    new[f].append(jnp.where(keep > 0.5, value, 0.0))
                else:
                    out_ref[f, i] = value
        if step < STEPS - 1:
            h, u, v = (jnp.stack(q) for q in new)


def local(n_st, n_ob, ensemble, weights, obs_column):
    rows, members = ensemble.shape
    obs = weights.shape[0]
    per = members // n_ob
    lats = rows // (FIELDS * NLON)
    chunk = obs // n_st
    vmem = pl.BlockSpec(memory_space=pltpu.VMEM)
    dma = pltpu.SemaphoreType.DMA
    ext = pl.pallas_call(
        functools.partial(analysis_kernel, n_st, n_ob),
        out_shape=jax.ShapeDtypeStruct((lats + 2 * STEPS, FIELDS, per, NLON), F32),
        in_specs=[pl.BlockSpec(memory_space=pltpu.HBM)] * 3,
        out_specs=vmem,
        scratch_shapes=[
            pltpu.VMEM((members, rows), BF16),
            pltpu.VMEM((members, obs), BF16),
            pltpu.VMEM((1, obs), jnp.int32),
            dma((3,)),
            pltpu.VMEM((members, rows), BF16),
            pltpu.VMEM((lats, FIELDS * NLON, members), BF16),
            pltpu.VMEM((obs, members), BF16),
            pltpu.VMEM((n_st, members, chunk), BF16),
            pltpu.VMEM((n_st, members, chunk), BF16),
            pltpu.VMEM((n_st, members, chunk), BF16),
            pltpu.VMEM((members, obs), BF16),
            pltpu.VMEM((lats, NLON, obs), F32),
            pltpu.VMEM((n_ob, lats, FIELDS, per, NLON), F32),
            pltpu.VMEM((n_ob, lats, FIELDS, per, NLON), BF16),
            pltpu.VMEM((n_ob, lats, FIELDS, per, NLON), BF16),
            dma((n_st,)), dma((n_st,)), dma((n_st,)), dma((n_st,)),
            dma((n_ob, lats)), dma((n_ob, lats)), dma((2,)), dma((2,)),
        ],
        compiler_params=pltpu.CompilerParams(
            collective_id=0, has_side_effects=True, vmem_limit_bytes=48 * 1024 * 1024
        ),
        name="analysis",
    )(ensemble.T, weights.T, obs_column.reshape(1, obs))
    lat_count = lats * n_st
    degrees = (np.arange(lat_count, dtype=np.float32) + 0.5) / lat_count - 0.5
    coriolis = (0.8 * np.sin(np.pi * degrees)).astype(np.float32).reshape(1, lat_count)
    fields = pl.pallas_call(
        functools.partial(forecast_kernel, n_st),
        out_shape=jax.ShapeDtypeStruct((FIELDS, lats, per, NLON), F32),
        in_specs=[pl.BlockSpec(memory_space=pltpu.SMEM), vmem],
        out_specs=vmem,
        compiler_params=pltpu.CompilerParams(vmem_limit_bytes=8 * 1024 * 1024),
        name="forecast",
    )(jnp.asarray(coriolis), ext)
    return fields.transpose(2, 0, 1, 3)


def solution(mesh):
    return jax.shard_map(
        functools.partial(local, mesh.shape["st"], mesh.shape["ob"]),
        mesh=mesh,
        in_specs=(P("st", None), P("ob", None), P("ob")),
        out_specs=P("ob", None, "st", None),
        check_vma=False,
    )
```

```python
import functools

import jax
import jax.numpy as jnp
from jax import lax
from jax.experimental import pallas as pl
from jax.experimental.pallas import tpu as pltpu
from jax.sharding import PartitionSpec as P

NLON = 128
FIELDS = 3
STEPS = 3
MESH = pl.DeviceIdType.MESH
time_step = 0.3
F32 = jnp.float32
BF16 = jnp.bfloat16


def remote(src, dst, send, recv, device):
    return pltpu.make_async_remote_copy(
        src_ref=src, dst_ref=dst, send_sem=send, recv_sem=recv, device_id=device, device_id_type=MESH
    )


def analysis_kernel(
    n_st, n_ob, ens_hbm, w_hbm, col_hbm, out_ref, ens_ref, w_ref, col_ref, loaded,
    anom_t, anom, w, picked, part, gathered, obs_t, taper, acc, inc, inc_send, inc_recv,
    ext, halo_send, halo_recv, turn, p_send, p_recv, g_send, g_recv, i_send, i_recv, h_send, h_recv,
):
    st, ob = lax.axis_index("st"), lax.axis_index("ob")
    members, rows = ens_ref.shape
    obs = w_ref.shape[1]
    per = members // n_ob
    lats = rows // (FIELDS * NLON)
    blocks = rows // NLON
    chunk = obs // n_st
    groups = obs_t.shape[0]
    width = obs // groups
    chunks = n_st // groups
    radius2 = float((lats * n_st) ** 2)

    loads = [
        pltpu.make_async_copy(src, dst, loaded.at[i])
        for i, (src, dst) in enumerate(((ens_hbm, ens_ref), (col_hbm, col_ref), (w_hbm, w_ref)))
    ]
    for load in loads:
        load.start()
    barrier = pltpu.get_barrier_semaphore()
    for d in range(1, n_st):
        pl.semaphore_signal(barrier, inc=1, device_id={"st": lax.rem(st + d, n_st)}, device_id_type=MESH)
    for d in range(1, n_ob):
        pl.semaphore_signal(barrier, inc=1, device_id={"ob": lax.rem(ob + d, n_ob)}, device_id_type=MESH)

    loads[0].wait()
    for b in range(blocks):
        e_t = ens_ref[:, b * NLON:(b + 1) * NLON].astype(F32)
        mean = jnp.sum(e_t, axis=0, keepdims=True) / members
        anom_t[:, b * NLON:(b + 1) * NLON] = (e_t - mean).astype(BF16)

    loads[1].wait()
    column = col_ref[...]
    depth = 2 * FIELDS * NLON if lats % 2 == 0 else FIELDS * NLON
    relative = column - st * rows
    spot = lax.broadcasted_iota(jnp.int32, (depth, obs), 0)
    total = jnp.zeros((members, obs), F32)
    for k in range(rows // depth):
        hot = jnp.where(spot == relative - k * depth, F32(1.0), F32(0.0)).astype(BF16)
        total = total + jnp.dot(anom_t[:, k * depth:(k + 1) * depth], hot, preferred_element_type=F32)
    total = total.astype(BF16)
    for c in range(n_st):
        picked[c] = total[:, c * chunk:(c + 1) * chunk]

    pl.semaphore_wait(barrier, n_st - 1 + n_ob - 1)

    first = []
    for d in range(1, n_st):
        peer = lax.rem(st + d, n_st)
        first.append(remote(picked.at[peer], part.at[d], p_send.at[d], p_recv.at[d], {"st": peer}))
    for copy in first:
        copy.start()

    for b in range(blocks):
        l, f = divmod(b, FIELDS)
        block = anom_t[:, b * NLON:(b + 1) * NLON].astype(F32)
        anom[l, f * NLON:(f + 1) * NLON, :] = block.T.astype(BF16)
    loads[2].wait()
    for b in range(obs // NLON):
        at = slice(b * NLON, (b + 1) * NLON)
        g, i = divmod(b * NLON, width)
        w[g, i:i + NLON, :] = w_ref[:, at].astype(F32).T.astype(BF16)
    obs_lat = jnp.floor((column.astype(F32) + 0.5) * (1.0 / (FIELDS * NLON)))
    obs_lon = (column & (NLON - 1)).astype(F32)
    lon = lax.broadcasted_iota(jnp.int32, (NLON, obs), 0).astype(F32)
    lon_gap = jnp.abs(lon - obs_lon)
    lon_gap = jnp.minimum(lon_gap, NLON - lon_gap)
    lon_left = radius2 - lon_gap * lon_gap
    scale = 1.0 / (radius2 * radius2 * (members - 1))
    for l in range(lats):
        lat_gap = obs_lat - (st * lats + l).astype(F32)
        fall = jnp.maximum(lon_left - lat_gap * lat_gap, 0.0)
        fall = fall * (fall * scale)
        for g in range(groups):
            taper[g, l] = fall[:, g * width:(g + 1) * width]
    latitude = lax.broadcasted_iota(jnp.int32, turn.shape, 0) + (st * lats - STEPS)
    angle = (latitude.astype(F32) + 0.5) / (lats * n_st) - 0.5
    turn[...] = 0.8 * jnp.sin(jnp.pi * angle)

    for copy in first:
        copy.wait_recv()
    mine = picked[st].astype(F32)
    for d in range(1, n_st):
        mine = mine + part[d].astype(F32)
    gathered[st] = mine.astype(BF16)

    second = []
    for d in range(1, n_st):
        peer = lax.rem(st + d, n_st)
        second.append(remote(gathered.at[st], gathered.at[st], g_send.at[d], g_recv.at[st], {"st": peer}))
    for copy in second:
        copy.start()

    home = st // chunks

    def arrive(q):
        group = lax.rem(home + q, groups)
        for i in range(chunks):
            source = group * chunks + i

            @pl.when(source != st)
            def _():
                here = gathered.at[source]
                remote(here, here, g_send.at[0], g_recv.at[source], {"st": source}).wait_recv()

            obs_t[q, :, i * chunk:(i + 1) * chunk] = gathered[source]
        return group

    def product(q, group, l):
        cov = jnp.dot(anom[l], obs_t[q], preferred_element_type=F32)
        gain = cov.reshape(FIELDS, NLON, width) * taper[group, l][None]
        gain = gain.astype(BF16).reshape(FIELDS * NLON, width)
        return jnp.dot(gain, w[group], preferred_element_type=F32)

    together = 3 if lats % 3 == 0 else 1
    for q in range(groups - 1):
        group = arrive(q)

        def some(i, carry):
            for j in range(together):
                l = i * together + j
                value = product(q, group, l)
                acc[l] = value if q == 0 else acc[l] + value
            return carry

        lax.fori_loop(0, lats // together, some, 0)
    last = arrive(groups - 1)

    def sends(l):
        return [
            remote(
                inc_send.at[lax.rem(ob + d, n_ob), l], inc_recv.at[d, l],
                i_send.at[d, l], i_recv.at[d, l], {"ob": lax.rem(ob + d, n_ob)},
            )
            for d in range(1, n_ob)
        ]

    def finish(l, carry):
        total = acc[l] + product(groups - 1, last, l)
        for f in range(FIELDS):
            turned = total[f * NLON:(f + 1) * NLON, :].T.reshape(n_ob, per, NLON)
            inc[:, l, f] = turned
            inc_send[:, l, f] = turned.astype(BF16)
        for copy in sends(l):
            copy.start()
        return carry

    lax.fori_loop(0, lats, finish, 0)

    own = ens_ref[pl.ds(pl.multiple_of(ob * per, per), per), :].astype(F32)
    for l in range(lats):
        for copy in sends(l):
            copy.wait_recv()
        for f in range(FIELDS):
            value = own[:, (l * FIELDS + f) * NLON:(l * FIELDS + f + 1) * NLON] + inc[ob, l, f]
            for d in range(1, n_ob):
                value = value + inc_recv[d, l, f].astype(F32)
            ext[STEPS + l, f] = value

    halo_send[0] = ext[lats:lats + STEPS].astype(BF16)
    halo_send[1] = ext[STEPS:2 * STEPS].astype(BF16)
    up = remote(halo_send.at[0], halo_recv.at[0], h_send.at[0], h_recv.at[0], {"st": lax.rem(st + 1, n_st)})
    down = remote(
        halo_send.at[1], halo_recv.at[1], h_send.at[1], h_recv.at[1], {"st": lax.rem(st + n_st - 1, n_st)}
    )

    @pl.when(st < n_st - 1)
    def _():
        up.start()

    @pl.when(st > 0)
    def _():
        down.start()

    for copy in first + second:
        copy.wait_send()
    for l in range(lats):
        for copy in sends(l):
            copy.wait_send()
    edge = jnp.zeros((STEPS,) + ext.shape[1:], F32)

    @pl.when(st == 0)
    def _():
        ext[0:STEPS] = edge

    @pl.when(st == n_st - 1)
    def _():
        ext[STEPS + lats:] = edge

    @pl.when(st < n_st - 1)
    def _():
        up.wait_send()
        down.wait_recv()
        ext[STEPS + lats:] = halo_recv[1].astype(F32)

    @pl.when(st > 0)
    def _():
        down.wait_send()
        up.wait_recv()
        ext[0:STEPS] = halo_recv[0].astype(F32)

    forecast(st, lats, lats * n_st, ext, turn, out_ref)


def forecast(st, lats, lat_count, ext, turn, out_ref):
    def east(q):
        return pltpu.roll(q, NLON - 1, 2)

    def west(q):
        return pltpu.roll(q, 1, 2)

    h, u, v = (ext[:, f] for f in range(FIELDS))
    for step in range(STEPS):
        flux_east = (1.0 + h[1:-1]) * u[1:-1]
        flux_north = (1.0 + h) * v
        around, dlon, dlat = [], [], []
        for q in (h, u, v):
            c = q[1:-1]
            e, w, n, s = east(c), west(c), q[2:], q[:-2]
            around.append(0.25 * (n + s + e + w))
            dlon.append((e - w) * 0.5)
            dlat.append((n - s) * 0.5)
        divergence = (east(flux_east) - west(flux_east)) * 0.5 + (flux_north[2:] - flux_north[:-2]) * 0.5
        cu, cv = u[1:-1], v[1:-1]
        count = cu.shape[0]
        base = st * lats - STEPS + step + 1
        new = [[], [], []]
        for i in range(count):
            latitude = base + i
            inside = (latitude >= 0) & (latitude < lat_count)
            keep = jnp.where(inside, F32(1.0), F32(0.0))
            force = turn[step + 1 + i:step + 2 + i, :]
            tend_u = cu[i] * dlon[1][i] + cv[i] * dlat[1][i] + dlon[0][i] - force * cv[i]
            tend_v = cu[i] * dlon[2][i] + cv[i] * dlat[2][i] + dlat[0][i] + force * cu[i]
            for f, tend in enumerate((divergence[i], tend_u, tend_v)):
                value = around[f][i] - time_step * tend
                if step < STEPS - 1:
                    new[f].append(jnp.where(keep > 0.5, value, 0.0))
                else:
                    out_ref[f, i] = value
        if step < STEPS - 1:
            h, u, v = (jnp.stack(q) for q in new)


def local(n_st, n_ob, ensemble, weights, obs_column):
    rows, members = ensemble.shape
    obs = weights.shape[0]
    per = members // n_ob
    lats = rows // (FIELDS * NLON)
    chunk = obs // n_st
    groups = 4 if n_st % 4 == 0 and obs % (4 * NLON) == 0 else 1
    vmem = pl.BlockSpec(memory_space=pltpu.VMEM)
    dma = pltpu.SemaphoreType.DMA
    fields = pl.pallas_call(
        functools.partial(analysis_kernel, n_st, n_ob),
        out_shape=jax.ShapeDtypeStruct((FIELDS, lats, per, NLON), F32),
        in_specs=[pl.BlockSpec(memory_space=pltpu.HBM)] * 3,
        out_specs=vmem,
        scratch_shapes=[
            pltpu.VMEM((members, rows), BF16),
            pltpu.VMEM((members, obs), BF16),
            pltpu.VMEM((1, obs), jnp.int32),
            dma((3,)),
            pltpu.VMEM((members, rows), BF16),
            pltpu.VMEM((lats, FIELDS * NLON, members), BF16),
            pltpu.VMEM((groups, obs // groups, members), BF16),
            pltpu.VMEM((n_st, members, chunk), BF16),
            pltpu.VMEM((n_st, members, chunk), BF16),
            pltpu.VMEM((n_st, members, chunk), BF16),
            pltpu.VMEM((groups, members, obs // groups), BF16),
            pltpu.VMEM((groups, lats, NLON, obs // groups), F32),
            pltpu.VMEM((lats, FIELDS * NLON, members), F32),
            pltpu.VMEM((n_ob, lats, FIELDS, per, NLON), F32),
            pltpu.VMEM((n_ob, lats, FIELDS, per, NLON), BF16),
            pltpu.VMEM((n_ob, lats, FIELDS, per, NLON), BF16),
            pltpu.VMEM((lats + 2 * STEPS, FIELDS, per, NLON), F32),
            pltpu.VMEM((2, STEPS, FIELDS, per, NLON), BF16),
            pltpu.VMEM((2, STEPS, FIELDS, per, NLON), BF16),
            pltpu.VMEM((-(lats + 2 * STEPS) // 8 * -8, NLON), F32),
            dma((n_st,)), dma((n_st,)), dma((n_st,)), dma((n_st,)),
            dma((n_ob, lats)), dma((n_ob, lats)), dma((2,)), dma((2,)),
        ],
        compiler_params=pltpu.CompilerParams(
            collective_id=0, has_side_effects=True, vmem_limit_bytes=48 * 1024 * 1024
        ),
        name="analysis",
    )(*(pltpu.with_memory_space_constraint(x, pltpu.HBM) for x in (ensemble.T, weights.T, obs_column.reshape(1, obs))))
    return fields.transpose(2, 0, 1, 3)


def solution(mesh):
    return jax.shard_map(
        functools.partial(local, mesh.shape["st"], mesh.shape["ob"]),
        mesh=mesh,
        in_specs=(P("st", None), P("ob", None), P("ob")),
        out_specs=P("ob", None, "st", None),
        check_vma=False,
    )
```
